32 devices in a mesh: orb: 8 (over y, x, core), slab: 4 (over z).
Axes of the slice: x: 2, y: 2, z: 4, core: 2. Of those that a mesh axis runs over, the one named last changes fastest.
Arguments:
- orbitals: float32 [8, 2, 128, 32, 128], P('orb', None, None, 'slab'), may hold values from -7 to 7, as said below
- potential: float32 [128, 32, 128], P(None, 'slab'), may hold values from 0 to 2
- occupation: float32 [8], P('orb'), may hold values from 0.5 to 2
- e_field: float32 [3, 128, 32, 128], P(None, 'orb', 'slab'), may hold values from -3 to 3
- a_field: float32 [3, 128, 32, 128], P(None, 'orb', 'slab'), may hold values from -1.8 to 1.8
Outputs:
- orbitals_next: float32 [8, 2, 128, 32, 128], P('orb', None, None, 'slab')
- electric_field: float32 [3, 128, 32, 128], P(None, 'orb', 'slab')
- vector_potential: float32 [3, 128, 32, 128], P(None, 'orb', 'slab')
The draws below stay inside these ranges and needn't reach their ends.
Inputs may be any that keep to these rules, and one draw needn't show every extreme that they name: `orbitals`: real and imaginary parts of each orbital at each cell.
All inputs are finite; a program needn't handle non-finite values.
Results may differ from the reference program's by a relative error of at most 0.0003.
Values sent between devices are 32-bit elements; how exact they have to be, the bound alone decides.
A program may use at most 64 MiB of HBM per device.

```python
import math
import jax
import jax.numpy as jnp
from jax import lax

ORBS = 8
NX = 128
NY = 128
NZ = 32
TERMS = 4
STEPS = 2


def draw_orbitals(key, part):
    depth = jnp.arange(NZ).astype(jnp.float32) / (NZ - 1)
    shape = (ORBS, 2, NX, NZ, NY)
    values = jnp.clip(jax.random.normal(key, shape, jnp.float32), -4.0, 4.0)
    ramp = jnp.sqrt(1.0 + 2.0 * depth)
    return values * ramp[None, None, None, :, None]


def levels(key, shape, pieces, least, high):
    gain, own = 1.0, jax.random.fold_in(key, 6)
    for dim, shards_of in pieces:
        heights = jnp.exp(jax.random.uniform(jax.random.fold_in(own, dim), (shards_of,), jnp.float32, least / len(pieces), high / len(pieces)))
        gain = gain * jnp.repeat(heights, shape[dim] // shards_of).reshape([-1 if axis == dim else 1 for axis in range(len(shape))])
    return gain


def centred(own_key, shape, width, reach, split=(), held_as=jnp.bfloat16):
    drawn = width * jax.random.normal(own_key, shape, jnp.float32)
    if split:
        drawn = drawn * levels(own_key, shape, split, -0.22, 0.18)
    return jnp.clip(drawn, -reach, reach).astype(held_as)


def setup_inputs(seed: int = 0) -> dict:
    splits = jax.random.split(jax.random.key(seed), 6)
    return {
        "orbitals": draw_orbitals(jax.random.fold_in(splits[5], 71), 0),
        "potential": jnp.clip(2.0 * jax.random.uniform(splits[1], (NX, NZ, NY), jnp.float32) ** levels(splits[1], (NX, NZ, NY), ((1, 4),), -0.2, 0.2), 0.0, 2.0),
        "occupation": jnp.clip(jnp.exp(math.log(2.0) - 1.3862944 * jax.random.uniform(splits[2], (ORBS,), jnp.float32) ** levels(splits[2], (ORBS,), ((0, 8),), -0.2, 0.2)), 0.5, 2.0),
        "e_field": centred(splits[3], (3, NX, NZ, NY), 0.5, 3.0, ((1, 8), (2, 4)), jnp.float32),
        "a_field": centred(splits[4], (3, NX, NZ, NY), 0.3, 1.8, ((1, 8), (2, 4)), jnp.float32),
    }


time_step = 0.3
wave_step = 0.5
epsilon = 1e-06

def trim_axis(array, axis, start, stop):
    return lax.slice_in_dim(array, start, array.shape[axis] + stop, axis=axis)

def forward(field, axis):
    diff = trim_axis(field, axis, 1, 0) - trim_axis(field, axis, 0, -1)
    for other in (0, 1, 2):
        if other != axis:
            diff = trim_axis(diff, other, 0, -1)
    return diff

def backward(field, axis):
    diff = trim_axis(field, axis, 1, 0) - trim_axis(field, axis, 0, -1)
    for other in (0, 1, 2):
        if other != axis:
            diff = trim_axis(diff, other, 1, 0)
    return diff

def curl_of(field, differ):
    comp_x, comp_y, comp_z = (field[0], field[1], field[2])
    out_x = differ(comp_z, 2) - differ(comp_y, 1)
    out_y = differ(comp_x, 1) - differ(comp_z, 0)
    out_z = differ(comp_y, 0) - differ(comp_x, 2)
    return jnp.stack([out_x, out_y, out_z])

def double_curl(padded):
    return curl_of(curl_of(padded, forward), backward)

def neighbours(padded):
    center = padded[:, :, 1:-1, 1:-1, 1:-1]
    x_plus = padded[:, :, 2:, 1:-1, 1:-1]
    x_minus = padded[:, :, :-2, 1:-1, 1:-1]
    z_plus = padded[:, :, 1:-1, 2:, 1:-1]
    z_minus = padded[:, :, 1:-1, :-2, 1:-1]
    y_plus = padded[:, :, 1:-1, 1:-1, 2:]
    y_minus = padded[:, :, 1:-1, 1:-1, :-2]
    return (center, (x_plus, x_minus), (y_plus, y_minus), (z_plus, z_minus))

def hamiltonian(padded, field, weight):
    center, along_x, along_y, along_z = neighbours(padded)
    laplace = along_x[0] + along_x[1] + along_y[0] + along_y[1] + along_z[0] + along_z[1] - 6.0 * center
    drift = 0.5 * (field[0] * (along_x[0] - along_x[1]) + field[1] * (along_y[0] - along_y[1]) + field[2] * (along_z[0] - along_z[1]))
    real_h = -0.5 * laplace[:, 0] + drift[:, 1] + weight * center[:, 0]
    imag_h = -0.5 * laplace[:, 1] - drift[:, 0] + weight * center[:, 1]
    return (real_h, imag_h)

def taylor_term(real_h, imag_h, order):
    factor = time_step / order
    return jnp.stack([factor * imag_h, -factor * real_h], axis=1)

def current_density(padded, field, weights):
    center, along_x, along_y, along_z = neighbours(padded)
    real_c = center[:, 0]
    imag_c = center[:, 1]
    density = real_c * real_c + imag_c * imag_c
    parts = []
    for pair, comp in ((along_x, 0), (along_y, 1), (along_z, 2)):
        grad_r = 0.5 * (pair[0][:, 0] - pair[1][:, 0])
        grad_i = 0.5 * (pair[0][:, 1] - pair[1][:, 1])
        flow = real_c * grad_i - imag_c * grad_r + field[comp] * density
        parts.append(lax.optimization_barrier(jnp.sum(weights[:, None, None, None] * flow, axis=0)))
    return jnp.stack(parts)

def pad_all(array):
    return jnp.pad(array, ((0, 0), (0, 0), (1, 1), (1, 1), (1, 1)))

def reference(orbitals, potential, occupation, e_field, a_field):
    cells = NX * NZ * NY
    e_state = e_field
    a_state = a_field
    for step in range(STEPS):
        field = a_state
        weight = potential + 0.5 * lax.optimization_barrier(jnp.sum(field * field, axis=0))

        def advance(flow, item):
            orbital, occ = item
            block = orbital[None]
            total = block
            term = block
            for order in range(1, TERMS + 1):
                real_h, imag_h = hamiltonian(pad_all(term), field, weight)
                term = taylor_term(real_h, imag_h, order)
                total = total + term
            norm = jnp.sum(total * total)
            scale = 1.0 / jnp.sqrt(norm / cells + epsilon)
            normed = total * scale
            weights = (occ * (1.0 / ORBS))[None]
            flow = flow + current_density(pad_all(normed), field, weights)
            return (flow, normed[0])
        start = jnp.zeros((3, NX, NZ, NY), jnp.float32)
        flow, orbitals = lax.scan(advance, start, (orbitals, occupation))
        padded = jnp.pad(a_state, ((0, 0), (1, 1), (1, 1), (1, 1)))
        e_state = e_state + wave_step * (double_curl(padded) - flow)
        a_state = a_state - wave_step * e_state
    return (orbitals, e_state, a_state)
```

```python
import functools

import jax
import jax.numpy as jnp
from jax import lax
from jax.experimental import pallas as pl
from jax.experimental.pallas import tpu as pltpu
from jax.sharding import PartitionSpec as P

TERMS = 4
STEPS = 2

time_step = 0.3
wave_step = 0.5
epsilon = 1e-06

MESH = pl.DeviceIdType.MESH
F32 = jnp.float32


def kernel(
    n_orb,
    n_slab,
    orb_ref,
    pot_ref,
    occ_ref,
    e_ref,
    a_ref,
    out_ref,
    eout_ref,
    aout_ref,
    ta,
    tb,
    tot,
    w3,
    af,
    azb,
    sb,
    hz,
    cr,
    hs,
    azs,
    azr,
    enew,
    anew,
    jmine,
    jsend,
    prx,
    jsum,
    rsx,
    nbs,
    nbr,
    ag_s,
    ag_r,
    fw_s,
    fw_r,
    hz_s,
    hz_r,
    az_s,
    az_r,
    pr_s,
    pr_r,
    rs_s,
    rs_r,
    nb_s,
    nb_r,
):
    groups = n_orb // 2
    _, _, nx, zb, ny = orb_ref.shape
    xb = a_ref.shape[1]
    xc = 8 if nx % 8 == 0 and xb % 8 == 0 else xb
    cells = nx * zb * n_slab * ny
    me = lax.axis_index("orb")
    me_s = lax.axis_index("slab")
    me_g = me // 2
    core = me % 2
    partner = me_g * 2 + (1 - core)
    has = (me_s > 0, me_s < n_slab - 1)
    nbr_dev = (me_s - 1, me_s + 1)

    barrier = pltpu.get_barrier_semaphore()

    def greet(o, s):
        pl.semaphore_signal(barrier, inc=1, device_id=(o, s), device_id_type=MESH)

    def group(d):
        return lax.rem(me_g + d, groups)

    def source(d):
        return lax.rem(me_g + groups - d, groups)

    greet(partner, me_s)
    for d in range(1, groups):
        greet(group(d) * 2 + core, me_s)
    for d in range(1, n_slab):
        greet(me, lax.rem(me_s + d, n_slab))

    row = lax.broadcasted_iota(jnp.int32, (1, zb, ny), 1)
    lane = lax.broadcasted_iota(jnp.int32, (1, zb, ny), 2)
    edge = (row == 0, row == zb - 1)
    first_lane, last_lane = lane == 0, lane == ny - 1
    sends = []

    def remote(src, dst, ss, rs, o, s):
        return pltpu.make_async_remote_copy(
            src_ref=src, dst_ref=dst, send_sem=ss, recv_sem=rs, device_id=(o, s), device_id_type=MESH
        )

    def y_next(v):
        return jnp.where(last_lane, 0.0, pltpu.roll(v, ny - 1, 2))

    def y_prev(v):
        return jnp.where(first_lane, 0.0, pltpu.roll(v, 1, 2))

    def z_next(v, halo=0.0):
        return jnp.where(edge[1], halo, pltpu.roll(v, zb - 1, 1))

    def z_prev(v, halo=0.0):
        return jnp.where(edge[0], halo, pltpu.roll(v, 1, 1))

    def halo_copy(h, side):
        return remote(
            sb.at[h, side], hz.at[h, 1 - side], hz_s.at[h, side], hz_r.at[h, 1 - side], me, nbr_dev[side]
        )

    def send_halo(h):
        for side in range(2):

            @pl.when(has[side])
            def _():
                halo_copy(h, side).start()

    def wait_halo(h):
        for side in range(2):

            @pl.when(has[side])
            def _():
                remote(
                    sb.at[h, side], hz.at[h, side], hz_s.at[h, side], hz_r.at[h, side], me, nbr_dev[side]
                ).wait_recv()

    def wait_halo_sent(h):
        for side in range(2):

            @pl.when(has[side])
            def _():
                halo_copy(h, side).wait_send()

    zero_x = jnp.zeros((zb, ny), F32)
    for buf in (ta, tb, tot):
        for part in range(2):
            buf[part, 0] = zero_x
            buf[part, nx + 1] = zero_x
    for step in range(STEPS):
        for comp in range(3):
            af[step, comp, 0] = zero_x
            af[step, comp, nx + 1] = zero_x

    def load_start(i, carry):
        for part in range(2):
            v = orb_ref[0, part, pl.ds(i * xc, xc)]
            ta[part, pl.ds(1 + i * xc, xc)] = v
            tot[part, pl.ds(1 + i * xc, xc)] = v
            sb[0, 0, part, pl.ds(i * xc, xc)] = v[:, 0, :]
            sb[0, 1, part, pl.ds(i * xc, xc)] = v[:, zb - 1, :]
        return carry

    lax.fori_loop(0, nx // xc, load_start, 0)

    for side in range(2):

        @pl.when(jnp.logical_not(has[side]))
        def _():
            for h in range(STEPS * (TERMS + 1)):
                hz[h, side] = jnp.zeros(hz.shape[2:], F32)
            for step in range(STEPS):
                azr[step, side] = jnp.zeros(azr.shape[2:], F32)

    pl.semaphore_wait(barrier, 1 + (groups - 1) + (n_slab - 1))

    def block(o):
        return pl.ds(1 + o * xb, xb)

    def gather_fields(step, src):
        copies = []
        for d in range(1, groups):
            c = remote(src, af.at[step, :, block(me)], ag_s.at[step, d], ag_r.at[step, d], group(d) * 2 + core, me_s)
            c.start()
            sends.append(c)
        c = remote(src, af.at[step, :, block(me)], fw_s.at[step, 0], fw_r.at[step, 0], partner, me_s)
        c.start()
        sends.append(c)

    def weigh(step, o):
        def rows(i, carry):
            x = o * xb + i * xc
            a = [af[step, comp, pl.ds(1 + x, xc)] for comp in range(3)]
            w3[pl.ds(x, xc)] = (
                pot_ref[pl.ds(x, xc)] + 0.5 * (a[0] * a[0] + a[1] * a[1] + a[2] * a[2]) + 3.0
            )
            azb[0, pl.ds(x, xc)] = a[2][:, 0, :]
            azb[1, pl.ds(x, xc)] = a[2][:, zb - 1, :]
            return carry

        lax.fori_loop(0, xb // xc, rows, 0)

    def finish_gather(step, src):
        for comp in range(3):
            af[step, comp, block(me)] = src[comp]
        weigh(step, me)
        for d in range(1, groups):
            o = source(d) * 2 + core
            remote(
                src, af.at[step, :, block(o)], ag_s.at[step, d], ag_r.at[step, d], group(d) * 2 + core, me_s
            ).wait_recv()
            c = remote(
                af.at[step, :, block(o)], af.at[step, :, block(o)], fw_s.at[step, d], fw_r.at[step, d], partner, me_s
            )
            c.start()
            sends.append(c)
            weigh(step, o)
        for d in range(groups):
            o = source(d) * 2 + (1 - core)
            remote(
                af.at[step, :, block(o)], af.at[step, :, block(o)], fw_s.at[step, d], fw_r.at[step, d], partner, me_s
            ).wait_recv()
            weigh(step, o)

    def az_copy(step, side):
        return remote(
            azs.at[step, side],
            azr.at[step, 1 - side],
            az_s.at[step, side],
            az_r.at[step, 1 - side],
            me,
            nbr_dev[side],
        )

    def send_az(step):
        for comp in range(3):
            v = af[step, comp, pl.ds(me * xb, xb + 2)]
            azs[step, 0, comp] = v[:, 0, :]
            azs[step, 1, comp] = v[:, zb - 1, :]
        for side in range(2):

            @pl.when(has[side])
            def _():
                az_copy(step, side).start()

    def half_fields(step, e_src):
        for side in range(2):

            @pl.when(has[side])
            def _():
                remote(
                    azs.at[step, side],
                    azr.at[step, side],
                    az_s.at[step, side],
                    az_r.at[step, side],
                    me,
                    nbr_dev[side],
                ).wait_recv()

        def rows(i, carry):
            x = me * xb + 1 + i

            def at(comp, dx):
                return af[step, comp, pl.ds(x + dx, 1)]

            def up(comp, dx):
                return z_next(at(comp, dx), azr[step, 1, comp, pl.ds(1 + i + dx, 1)][:, None, :])

            def down(comp, dx):
                return z_prev(at(comp, dx), azr[step, 0, comp, pl.ds(1 + i + dx, 1)][:, None, :])

            ax, ay, az = at(0, 0), at(1, 0), at(2, 0)
            ax_m, ay_p, az_p = at(0, -1), at(1, 1), at(2, 1)
            c_x = (
                (ay_p - ay - y_prev(ay_p) + y_prev(ay))
                + (az_p - az - down(2, 1) + down(2, 0))
                - (y_next(ax) + y_prev(ax) + up(0, 0) + down(0, 0) - 4.0 * ax)
            )
            c_y = (
                (y_next(ax) - ax - y_next(ax_m) + ax_m)
                + (y_next(az) - az - y_next(down(2, 0)) + down(2, 0))
                - (ay_p + at(1, -1) + up(1, 0) + down(1, 0) - 4.0 * ay)
            )
            c_z = (
                (up(0, 0) - ax - up(0, -1) + ax_m)
                + (up(1, 0) - ay - y_prev(up(1, 0)) + y_prev(ay))
                - (az_p + at(2, -1) + y_next(az) + y_prev(az) - 4.0 * az)
            )
            for comp, c in enumerate((c_x, c_y, c_z)):
                enew[step, comp, pl.ds(i, 1)] = e_src[comp, pl.ds(i, 1)] + wave_step * c
            return carry

        lax.fori_loop(0, xb, rows, 0)

    def bulk(step, order, t, tn, h):
        f = time_step / order

        def rows(i, carry):
            x = i * xc
            field = [af[step, comp, pl.ds(1 + x, xc)] for comp in range(3)]
            wt = w3[pl.ds(x, xc)]
            mid, total, drift = [], [], []
            for part in range(2):
                v = t[part, pl.ds(1 + x, xc)]
                xp, xm = t[part, pl.ds(2 + x, xc)], t[part, pl.ds(x, xc)]
                yp, ym = y_next(v), y_prev(v)
                zp, zm = z_next(v), z_prev(v)
                mid.append(v)
                total.append((xp + xm) + (yp + ym) + (zp + zm))
                drift.append(field[0] * (xp - xm) + field[1] * (yp - ym) + field[2] * (zp - zm))
            new_p = f * (wt * mid[1]) - (0.5 * f) * (total[1] + drift[0])
            new_q = (0.5 * f) * (total[0] - drift[1]) - f * (wt * mid[0])
            for part, new in enumerate((new_p, new_q)):
                tn[part, pl.ds(1 + x, xc)] = new
                sb[h, 0, part, pl.ds(x, xc)] = new[:, 0, :]
                sb[h, 1, part, pl.ds(x, xc)] = new[:, zb - 1, :]
            return carry

        lax.fori_loop(0, nx // xc, rows, 0)

    def correct(order, h_in, h_out):
        f = time_step / order
        for side in range(2):
            sign = 2.0 * side - 1.0
            hp, hq, az = hz[h_in, side, 0], hz[h_in, side, 1], azb[side]
            dp = (-0.5 * f) * (hq + sign * az * hp)
            dq = (0.5 * f) * (hp - sign * az * hq)
            cr[side, 0] = dp
            cr[side, 1] = dq
            sb[h_out, side, 0] = sb[h_out, side, 0] + dp
            sb[h_out, side, 1] = sb[h_out, side, 1] + dq

    def fix(tn):
        def rows(i, acc):
            x = i * xc
            for part in range(2):
                low = cr[0, part, pl.ds(x, xc)][:, None, :]
                high = cr[1, part, pl.ds(x, xc)][:, None, :]
                v = tn[part, pl.ds(1 + x, xc)] + jnp.where(edge[0], low, jnp.where(edge[1], high, 0.0))
                tn[part, pl.ds(1 + x, xc)] = v
                s = tot[part, pl.ds(1 + x, xc)] + v
                tot[part, pl.ds(1 + x, xc)] = s
                acc = acc + jnp.sum(s * s, axis=0)
            return acc

        return lax.fori_loop(0, nx // xc, rows, jnp.zeros((zb, ny), F32))

    def current(step, o, s2h, dst):
        def rows(i, carry):
            x = o * xb + i * xc
            mids, diffs = [], []
            for part in range(2):
                v = tot[part, pl.ds(1 + x, xc)]
                low = hs[0, part, pl.ds(x, xc)][:, None, :]
                high = hs[1, part, pl.ds(x, xc)][:, None, :]
                mids.append(v)
                diffs.append(
                    (
                        tot[part, pl.ds(2 + x, xc)] - tot[part, pl.ds(x, xc)],
                        y_next(v) - y_prev(v),
                        z_next(v, high) - z_prev(v, low),
                    )
                )
            u, w = mids
            density = 2.0 * (u * u + w * w)
            for comp in range(3):
                a = af[step, comp, pl.ds(1 + x, xc)]
                dst[comp, pl.ds(i * xc, xc)] = s2h * (
                    u * diffs[1][comp] - w * diffs[0][comp] + a * density
                )
            return carry

        lax.fori_loop(0, xb // xc, rows, 0)

    send_halo(0)
    gather_fields(0, a_ref)
    for step in range(STEPS):
        base = step * (TERMS + 1)
        a_src = a_ref if step == 0 else anew.at[0]
        e_src = e_ref if step == 0 else eout_ref
        finish_gather(step, a_src)
        send_az(step)
        t, tn = ta, tb
        for order in range(1, TERMS + 1):
            bulk(step, order, t, tn, base + order)
            if order > 1 or step == 0:
                wait_halo(base + order - 1)
            correct(order, base + order - 1, base + order)
            send_halo(base + order)
            norm_tile = fix(tn)
            if order == 1:
                half_fields(step, e_src)
            t, tn = tn, t
        nbs[step] = norm_tile
        for d in range(1, n_slab):
            c = remote(
                nbs.at[step], nbr.at[step, d], nb_s.at[step, d], nb_r.at[step, d], me, lax.rem(me_s + d, n_slab)
            )
            c.start()
            sends.append(c)
        for d in range(1, n_slab):
            remote(nbs.at[step], nbr.at[step, d], nb_s.at[step, d], nb_r.at[step, d], me, me_s).wait_recv()
            norm_tile = norm_tile + nbr[step, d]
        norm = jnp.sum(jnp.sum(norm_tile, axis=0, keepdims=True), axis=1, keepdims=True)
        scale = jnp.broadcast_to(1.0 / jnp.sqrt(norm / cells + epsilon), (zb, ny))
        s2h = (scale * scale * (0.5 * (occ_ref[0] * (1.0 / n_orb))))[None]
        wait_halo(base + TERMS)
        for side in range(2):
            for part in range(2):
                total = hz[base, side, part]
                for k in range(1, TERMS + 1):
                    total = total + hz[base + k, side, part]
                hs[side, part] = total
        order_d = list(range(1, groups)) + [0]
        for d in order_d:
            current(step, group(d) * 2 + (1 - core), s2h, jsend.at[step, d])
            c = remote(
                jsend.at[step, d], prx.at[step, d], pr_s.at[step, d], pr_r.at[step, d], partner, me_s
            )
            c.start()
            sends.append(c)
        for d in order_d:
            current(step, group(d) * 2 + core, s2h, jmine.at[d])
            remote(
                jsend.at[step, d], prx.at[step, d], pr_s.at[step, d], pr_r.at[step, d], partner, me_s
            ).wait_recv()
            for comp in range(3):
                jsum[step, d, comp] = jmine[d, comp] + prx[step, d, comp]
            if d:
                c = remote(
                    jsum.at[step, d], rsx.at[step, d], rs_s.at[step, d], rs_r.at[step, d], group(d) * 2 + core, me_s
                )
                c.start()
                sends.append(c)

        def rescale(i, carry):
            x = i * xc
            for part in range(2):
                v = scale[None] * tot[part, pl.ds(1 + x, xc)]
                if step == STEPS - 1:
                    out_ref[0, part, pl.ds(x, xc)] = v
                else:
                    t[part, pl.ds(1 + x, xc)] = v
                    tot[part, pl.ds(1 + x, xc)] = v
            return carry

        lax.fori_loop(0, nx // xc, rescale, 0)
        if step < STEPS - 1:
            for side in range(2):
                for part in range(2):
                    hz[base + TERMS + 1, side, part] = scale[0:1] * hs[side, part]
        for d in range(1, groups):
            remote(
                jsum.at[step, d], rsx.at[step, d], rs_s.at[step, d], rs_r.at[step, d], partner, me_s
            ).wait_recv()

        for comp in range(3):
            flow = jsum[step, 0, comp]
            for d in range(1, groups):
                flow = flow + rsx[step, d, comp]
            e = enew[step, comp] - wave_step * flow
            eout_ref[comp] = e
            a = a_src[comp] - wave_step * e
            if step == STEPS - 1:
                aout_ref[comp] = a
            else:
                anew[step, comp] = a
        if step < STEPS - 1:
            gather_fields(step + 1, anew.at[step])

    for c in sends:
        c.wait_send()
    for h in range(STEPS * (TERMS + 1)):
        if h != TERMS + 1:
            wait_halo_sent(h)
    for step in range(STEPS):
        for side in range(2):

            @pl.when(has[side])
            def _():
                az_copy(step, side).wait_send()


def per_device(orbitals, potential, occupation, e_field, a_field):
    n_orb, n_slab = lax.axis_size("orb"), lax.axis_size("slab")
    _, _, nx, zb, ny = orbitals.shape
    xb = a_field.shape[1]
    groups = n_orb // 2
    halos = STEPS * (TERMS + 1)
    vmem = pl.BlockSpec(memory_space=pltpu.VMEM)

    def sem(*shape):
        return pltpu.SemaphoreType.DMA(shape)

    def buf(*shape):
        return pltpu.VMEM(shape, F32)

    return pl.pallas_call(
        functools.partial(kernel, n_orb, n_slab),
        out_shape=(
            jax.ShapeDtypeStruct(orbitals.shape, F32),
            jax.ShapeDtypeStruct(e_field.shape, F32),
            jax.ShapeDtypeStruct(a_field.shape, F32),
        ),
        in_specs=[vmem, vmem, pl.BlockSpec(memory_space=pltpu.SMEM), vmem, vmem],
        out_specs=(vmem, vmem, vmem),
        scratch_shapes=[
            buf(2, nx + 2, zb, ny),
            buf(2, nx + 2, zb, ny),
            buf(2, nx + 2, zb, ny),
            buf(nx, zb, ny),
            buf(STEPS, 3, nx + 2, zb, ny),
            buf(2, nx, ny),
            buf(halos, 2, 2, nx, ny),
            buf(halos, 2, 2, nx, ny),
            buf(2, 2, nx, ny),
            buf(2, 2, nx, ny),
            buf(STEPS, 2, 3, xb + 2, ny),
            buf(STEPS, 2, 3, xb + 2, ny),
            buf(STEPS, 3, xb, zb, ny),
            buf(STEPS, 3, xb, zb, ny),
            buf(groups, 3, xb, zb, ny),
            buf(STEPS, groups, 3, xb, zb, ny),
            buf(STEPS, groups, 3, xb, zb, ny),
            buf(STEPS, groups, 3, xb, zb, ny),
            buf(STEPS, groups, 3, xb, zb, ny),
            buf(STEPS, zb, ny),
            buf(STEPS, n_slab, zb, ny),
            sem(STEPS, groups),
            sem(STEPS, groups),
            sem(STEPS, groups),
            sem(STEPS, groups),
            sem(halos, 2),
            sem(halos, 2),
            sem(STEPS, 2),
            sem(STEPS, 2),
            sem(STEPS, groups),
            sem(STEPS, groups),
            sem(STEPS, groups),
            sem(STEPS, groups),
            sem(STEPS, n_slab),
            sem(STEPS, n_slab),
        ],
        compiler_params=pltpu.CompilerParams(
            collective_id=0, has_side_effects=True, vmem_limit_bytes=60 * 1024 * 1024
        ),
    )(orbitals, potential, occupation, e_field, a_field)


def solution(mesh):
    return jax.shard_map(
        per_device,
        mesh=mesh,
        in_specs=(
            P("orb", None, None, "slab", None),
            P(None, "slab", None),
            P("orb"),
            P(None, "orb", "slab", None),
            P(None, "orb", "slab", None),
        ),
        out_specs=(
            P("orb", None, None, "slab", None),
            P(None, "orb", "slab", None),
            P(None, "orb", "slab", None),
        ),
        check_vma=False,
    )
```

```python
import functools

import jax
import jax.numpy as jnp
from jax import lax
from jax.experimental import pallas as pl
from jax.experimental.pallas import tpu as pltpu
from jax.sharding import PartitionSpec as P

TERMS = 4
STEPS = 2

time_step = 0.3
wave_step = 0.5
epsilon = 1e-06

MESH = pl.DeviceIdType.MESH
F32 = jnp.float32


def kernel(
    n_orb,
    n_slab,
    orb_ref,
    pot_ref,
    occ_ref,
    e_ref,
    a_ref,
    out_ref,
    scale_ref,
    half_ref,
    flow_ref,
    aold_ref,
    ta,
    tb,
    tot,
    w3,
    af,
    sb,
    hz,
    hs,
    azs,
    azr,
    enew,
    ekeep,
    anew,
    jmine,
    jsend,
    prx,
    jsum,
    rsx,
    nbs,
    nbr,
    ag_s,
    ag_r,
    fw_s,
    fw_r,
    hz_s,
    hz_r,
    az_s,
    az_r,
    pr_s,
    pr_r,
    rs_s,
    rs_r,
    nb_s,
    nb_r,
):
    groups = n_orb // 2
    _, _, nx, zb, ny = orb_ref.shape
    xb = a_ref.shape[1]
    xc = 8 if nx % 8 == 0 and xb % 8 == 0 else xb
    cells = nx * zb * n_slab * ny
    me = lax.axis_index("orb")
    me_s = lax.axis_index("slab")
    me_g = me // 2
    core = me % 2
    partner = me_g * 2 + (1 - core)
    has = (me_s > 0, me_s < n_slab - 1)
    nbr_dev = (me_s - 1, me_s + 1)

    barrier = pltpu.get_barrier_semaphore()

    def greet(o, s):
        pl.semaphore_signal(barrier, inc=1, device_id=(o, s), device_id_type=MESH)

    def group(d):
        return lax.rem(me_g + d, groups)

    def source(d):
        return lax.rem(me_g + groups - d, groups)

    greet(partner, me_s)
    for d in range(1, groups):
        greet(group(d) * 2 + core, me_s)
    for d in range(1, n_slab):
        greet(me, lax.rem(me_s + d, n_slab))

    row = lax.broadcasted_iota(jnp.int32, (1, zb, ny), 1)
    lane = lax.broadcasted_iota(jnp.int32, (1, zb, ny), 2)
    edge = (row == 0, row == zb - 1)
    first_lane, last_lane = lane == 0, lane == ny - 1
    sends = []

    def remote(src, dst, ss, rs, o, s):
        return pltpu.make_async_remote_copy(
            src_ref=src, dst_ref=dst, send_sem=ss, recv_sem=rs, device_id=(o, s), device_id_type=MESH
        )

    def y_next(v):
        return jnp.where(last_lane, 0.0, pltpu.roll(v, ny - 1, 2))

    def y_prev(v):
        return jnp.where(first_lane, 0.0, pltpu.roll(v, 1, 2))

    def z_next(v, halo=0.0):
        return jnp.where(edge[1], halo, pltpu.roll(v, zb - 1, 1))

    def z_prev(v, halo=0.0):
        return jnp.where(edge[0], halo, pltpu.roll(v, 1, 1))

    def rows_of(o):
        return pl.ds(o * xb, xb)

    def halo_copy(h, side, o):
        return remote(
            sb.at[h, side, :, rows_of(o)],
            hz.at[h, 1 - side, :, rows_of(o)],
            hz_s.at[h, side, o],
            hz_r.at[h, 1 - side, o],
            me,
            nbr_dev[side],
        )

    def send_halo(h, o):
        for side in range(2):

            @pl.when(has[side])
            def _():
                halo_copy(h, side, o).start()

    def wait_halo(h, o):
        for side in range(2):

            @pl.when(has[side])
            def _():
                remote(
                    sb.at[h, side, :, rows_of(o)],
                    hz.at[h, side, :, rows_of(o)],
                    hz_s.at[h, side, o],
                    hz_r.at[h, side, o],
                    me,
                    nbr_dev[side],
                ).wait_recv()

    def wait_halo_sent(h, o):
        for side in range(2):

            @pl.when(has[side])
            def _():
                halo_copy(h, side, o).wait_send()

    zero_x = jnp.zeros((zb, ny), F32)
    for buf in (ta, tb, tot):
        for part in range(2):
            buf[part, 0] = zero_x
            buf[part, nx + 1] = zero_x
    for step in range(STEPS):
        for comp in range(3):
            af[step, comp, 0] = zero_x
            af[step, comp, nx + 1] = zero_x

    def load_start(o, carry):
        for i in range(xb // xc):
            x = o * xb + i * xc
            for part in range(2):
                v = orb_ref[0, part, pl.ds(x, xc)]
                ta[part, pl.ds(1 + x, xc)] = v
                sb[0, 0, part, pl.ds(x, xc)] = v[:, 0, :]
                sb[0, 1, part, pl.ds(x, xc)] = v[:, zb - 1, :]
        send_halo(0, o)
        return carry

    for side in range(2):

        @pl.when(jnp.logical_not(has[side]))
        def _():
            for h in range(STEPS * (TERMS + 1)):
                hz[h, side] = jnp.zeros(hz.shape[2:], F32)
            for step in range(STEPS):
                azr[step, side] = jnp.zeros(azr.shape[2:], F32)

    pl.semaphore_wait(barrier, 1 + (groups - 1) + (n_slab - 1))

    def block(o):
        return pl.ds(1 + o * xb, xb)

    def gather_fields(step, src):
        copies = []
        for d in range(1, groups):
            c = remote(src, af.at[step, :, block(me)], ag_s.at[step, d], ag_r.at[step, d], group(d) * 2 + core, me_s)
            c.start()
            sends.append(c)
        c = remote(src, af.at[step, :, block(me)], fw_s.at[step, 0], fw_r.at[step, 0], partner, me_s)
        c.start()
        sends.append(c)

    def weigh(step, o):
        def rows(i, carry):
            x = o * xb + i * xc
            a = [af[step, comp, pl.ds(1 + x, xc)] for comp in range(3)]
            w3[pl.ds(x, xc)] = (
                pot_ref[pl.ds(x, xc)] + 0.5 * (a[0] * a[0] + a[1] * a[1] + a[2] * a[2]) + 3.0
            )
            return carry

        lax.fori_loop(0, xb // xc, rows, 0)

    def finish_gather(step, src, use):
        for comp in range(3):
            af[step, comp, block(me)] = src[comp]
        weigh(step, me)
        use(me)
        for d in range(1, groups):
            o = source(d) * 2 + core
            remote(
                src, af.at[step, :, block(o)], ag_s.at[step, d], ag_r.at[step, d], group(d) * 2 + core, me_s
            ).wait_recv()
            c = remote(
                af.at[step, :, block(o)], af.at[step, :, block(o)], fw_s.at[step, d], fw_r.at[step, d], partner, me_s
            )
            c.start()
            sends.append(c)
            weigh(step, o)
            use(o)
        for d in range(groups):
            o = source(d) * 2 + (1 - core)
            remote(
                af.at[step, :, block(o)], af.at[step, :, block(o)], fw_s.at[step, d], fw_r.at[step, d], partner, me_s
            ).wait_recv()
            weigh(step, o)
            use(o)

    def az_copy(step, side):
        return remote(
            azs.at[step, side],
            azr.at[step, 1 - side],
            az_s.at[step, side],
            az_r.at[step, 1 - side],
            me,
            nbr_dev[side],
        )

    def send_az(step):
        for comp in range(3):
            v = af[step, comp, pl.ds(me * xb, xb + 2)]
            azs[step, 0, comp] = v[:, 0, :]
            azs[step, 1, comp] = v[:, zb - 1, :]
        for side in range(2):

            @pl.when(has[side])
            def _():
                az_copy(step, side).start()

    def half_fields(step, e_src):
        for side in range(2):

            @pl.when(has[side])
            def _():
                remote(
                    azs.at[step, side],
                    azr.at[step, side],
                    az_s.at[step, side],
                    az_r.at[step, side],
                    me,
                    nbr_dev[side],
                ).wait_recv()

        def rows(i, carry):
            x = me * xb + 1 + i

            def at(comp, dx):
                return af[step, comp, pl.ds(x + dx, 1)]

            def up(comp, dx):
                return z_next(at(comp, dx), azr[step, 1, comp, pl.ds(1 + i + dx, 1)][:, None, :])

            def down(comp, dx):
                return z_prev(at(comp, dx), azr[step, 0, comp, pl.ds(1 + i + dx, 1)][:, None, :])

            ax, ay, az = at(0, 0), at(1, 0), at(2, 0)
            ax_m, ay_p, az_p = at(0, -1), at(1, 1), at(2, 1)
            c_x = (
                (ay_p - ay - y_prev(ay_p) + y_prev(ay))
                + (az_p - az - down(2, 1) + down(2, 0))
                - (y_next(ax) + y_prev(ax) + up(0, 0) + down(0, 0) - 4.0 * ax)
            )
            c_y = (
                (y_next(ax) - ax - y_next(ax_m) + ax_m)
                + (y_next(az) - az - y_next(down(2, 0)) + down(2, 0))
                - (ay_p + at(1, -1) + up(1, 0) + down(1, 0) - 4.0 * ay)
            )
            c_z = (
                (up(0, 0) - ax - up(0, -1) + ax_m)
                + (up(1, 0) - ay - y_prev(up(1, 0)) + y_prev(ay))
                - (az_p + at(2, -1) + y_next(az) + y_prev(az) - 4.0 * az)
            )
            for comp, c in enumerate((c_x, c_y, c_z)):
                enew[step, comp, pl.ds(i, 1)] = e_src[comp, pl.ds(i, 1)] + wave_step * c
            return carry

        lax.fori_loop(0, xb, rows, 0)

    def term_block(step, order, t, tn, o, acc):
        f = time_step / order
        base = step * (TERMS + 1)
        h_in, h_out = base + order - 1, base + order
        if h_in != TERMS + 1:
            wait_halo(h_in, o)

        def rows(i, acc):
            x = o * xb + i * xc
            field = [af[step, comp, pl.ds(1 + x, xc)] for comp in range(3)]
            wt = w3[pl.ds(x, xc)]
            mid, total, drift = [], [], []
            for part in range(2):
                v = t[part, pl.ds(1 + x, xc)]
                xp, xm = t[part, pl.ds(2 + x, xc)], t[part, pl.ds(x, xc)]
                yp, ym = y_next(v), y_prev(v)
                zp = z_next(v, hz[h_in, 1, part, pl.ds(x, xc)][:, None, :])
                zm = z_prev(v, hz[h_in, 0, part, pl.ds(x, xc)][:, None, :])
                mid.append(v)
                total.append((xp + xm) + (yp + ym) + (zp + zm))
                drift.append(field[0] * (xp - xm) + field[1] * (yp - ym) + field[2] * (zp - zm))
            new_p = f * (wt * mid[1]) - (0.5 * f) * (total[1] + drift[0])
            new_q = (0.5 * f) * (total[0] - drift[1]) - f * (wt * mid[0])
            for part, new in enumerate((new_p, new_q)):
                sb[h_out, 0, part, pl.ds(x, xc)] = new[:, 0, :]
                sb[h_out, 1, part, pl.ds(x, xc)] = new[:, zb - 1, :]
                if order == 1:
                    s = mid[part] + new
                else:
                    s = tot[part, pl.ds(1 + x, xc)] + new
                tot[part, pl.ds(1 + x, xc)] = s
                if order < TERMS:
                    tn[part, pl.ds(1 + x, xc)] = new
                else:
                    acc = acc + jnp.sum(s * s, axis=0)
            return acc

        acc = lax.fori_loop(0, xb // xc, rows, acc)
        send_halo(h_out, o)
        return acc

    def current(step, o, s2h, dst):
        base = step * (TERMS + 1)
        wait_halo(base + TERMS, o)
        for side in range(2):
            for part in range(2):
                total = hz[base, side, part, rows_of(o)]
                for k in range(1, TERMS + 1):
                    total = total + hz[base + k, side, part, rows_of(o)]
                hs[side, part, rows_of(o)] = total

        def rows(i, carry):
            x = o * xb + i * xc
            mids, diffs = [], []
            for part in range(2):
                v = tot[part, pl.ds(1 + x, xc)]
                low = hs[0, part, pl.ds(x, xc)][:, None, :]
                high = hs[1, part, pl.ds(x, xc)][:, None, :]
                mids.append(v)
                diffs.append(
                    (
                        tot[part, pl.ds(2 + x, xc)] - tot[part, pl.ds(x, xc)],
                        y_next(v) - y_prev(v),
                        z_next(v, high) - z_prev(v, low),
                    )
                )
            u, w = mids
            density = 2.0 * (u * u + w * w)
            for comp in range(3):
                a = af[step, comp, pl.ds(1 + x, xc)]
                j = u * diffs[1][comp] - w * diffs[0][comp] + a * density
                dst[comp, pl.ds(i * xc, xc)] = j if s2h is None else s2h * j
            return carry

        lax.fori_loop(0, xb // xc, rows, 0)

    none = jnp.zeros((zb, ny), F32)
    order_d = list(range(1, groups)) + [0]
    gather_fields(0, a_ref)
    lax.fori_loop(0, n_orb, load_start, 0)
    for step in range(STEPS):
        base = step * (TERMS + 1)
        a_src = a_ref if step == 0 else anew.at[step - 1]
        e_src = e_ref if step == 0 else ekeep
        finish_gather(step, a_src, lambda o: term_block(step, 1, ta, tb, o, none))
        send_az(step)
        t, tn = tb, ta
        for order in range(2, TERMS):
            lax.fori_loop(
                0, n_orb, lambda o, acc: term_block(step, order, t, tn, o, acc), none
            )
            t, tn = tn, t

        def last(j, acc):
            side, d = j // groups, lax.rem(j % groups + 1, groups)
            other = side + core - 2 * side * core
            return term_block(step, TERMS, t, tn, group(d) * 2 + 1 - other, acc)

        norm_tile = lax.fori_loop(0, n_orb, last, none)
        nbs[step] = norm_tile
        for d in range(1, n_slab):
            c = remote(
                nbs.at[step], nbr.at[step, d], nb_s.at[step, d], nb_r.at[step, d], me, lax.rem(me_s + d, n_slab)
            )
            c.start()
            sends.append(c)
        for d in order_d:
            current(step, group(d) * 2 + (1 - core), None, jmine.at[d])
        for d in range(1, n_slab):
            remote(nbs.at[step], nbr.at[step, d], nb_s.at[step, d], nb_r.at[step, d], me, me_s).wait_recv()
            norm_tile = norm_tile + nbr[step, d]
        norm = jnp.sum(jnp.sum(norm_tile, axis=0, keepdims=True), axis=1, keepdims=True)
        scale = jnp.broadcast_to(1.0 / jnp.sqrt(norm / cells + epsilon), (zb, ny))
        s2h = (scale * scale * (0.5 * (occ_ref[0] * (1.0 / n_orb))))[None]
        for d in order_d:
            for comp in range(3):
                jsend[step, d, comp] = s2h * jmine[d, comp]
            c = remote(
                jsend.at[step, d], prx.at[step, d], pr_s.at[step, d], pr_r.at[step, d], partner, me_s
            )
            c.start()
            sends.append(c)
        for d in order_d:
            current(step, group(d) * 2 + core, s2h, jmine.at[d])
            remote(
                jsend.at[step, d], prx.at[step, d], pr_s.at[step, d], pr_r.at[step, d], partner, me_s
            ).wait_recv()
            for comp in range(3):
                jsum[step, d, comp] = jmine[d, comp] + prx[step, d, comp]
            if d:
                c = remote(
                    jsum.at[step, d], rsx.at[step, d], rs_s.at[step, d], rs_r.at[step, d], group(d) * 2 + core, me_s
                )
                c.start()
                sends.append(c)

        def rescale(i, carry):
            x = i * xc
            for part in range(2):
                v = tot[part, pl.ds(1 + x, xc)]
                if step == STEPS - 1:
                    out_ref[0, part, pl.ds(x, xc)] = v
                else:
                    ta[part, pl.ds(1 + x, xc)] = scale[None] * v
            return carry

        lax.fori_loop(0, nx // xc, rescale, 0)
        half_fields(step, e_src)
        if step < STEPS - 1:
            for side in range(2):
                for part in range(2):
                    hz[base + TERMS + 1, side, part] = scale[0:1] * hs[side, part]
        for d in range(1, groups):
            remote(
                jsum.at[step, d], rsx.at[step, d], rs_s.at[step, d], rs_r.at[step, d], partner, me_s
            ).wait_recv()

        for comp in range(3):
            flow = jsum[step, 0, comp]
            for d in range(1, groups):
                flow = flow + rsx[step, d, comp]
            if step == STEPS - 1:
                half_ref[comp] = enew[step, comp]
                flow_ref[comp] = flow
                aold_ref[comp] = a_src[comp]
            else:
                e = enew[step, comp] - wave_step * flow
                ekeep[comp] = e
                anew[step, comp] = a_src[comp] - wave_step * e
        if step < STEPS - 1:
            gather_fields(step + 1, anew.at[step])
        else:
            scale_ref[...] = scale

    for c in sends:
        c.wait_send()
    for h in range(STEPS * (TERMS + 1)):
        if h != TERMS + 1:
            lax.fori_loop(0, n_orb, lambda o, carry: (wait_halo_sent(h, o), carry)[1], 0)
    for step in range(STEPS):
        for side in range(2):

            @pl.when(has[side])
            def _():
                az_copy(step, side).wait_send()


def per_device(orbitals, potential, occupation, e_field, a_field):
    n_orb, n_slab = lax.axis_size("orb"), lax.axis_size("slab")
    _, _, nx, zb, ny = orbitals.shape
    xb = a_field.shape[1]
    groups = n_orb // 2
    halos = STEPS * (TERMS + 1)
    vmem = pl.BlockSpec(memory_space=pltpu.VMEM)

    def sem(*shape):
        return pltpu.SemaphoreType.DMA(shape)

    def buf(*shape):
        return pltpu.VMEM(shape, F32)

    moved, scale, half, flow, a_old = pl.pallas_call(
        functools.partial(kernel, n_orb, n_slab),
        out_shape=(
            jax.ShapeDtypeStruct(orbitals.shape, F32),
            jax.ShapeDtypeStruct((zb, ny), F32),
            jax.ShapeDtypeStruct(e_field.shape, F32),
            jax.ShapeDtypeStruct(e_field.shape, F32),
            jax.ShapeDtypeStruct(e_field.shape, F32),
        ),
        in_specs=[vmem, vmem, pl.BlockSpec(memory_space=pltpu.SMEM), vmem, vmem],
        out_specs=(vmem,) * 5,
        scratch_shapes=[
            buf(2, nx + 2, zb, ny),
            buf(2, nx + 2, zb, ny),
            buf(2, nx + 2, zb, ny),
            buf(nx, zb, ny),
            buf(STEPS, 3, nx + 2, zb, ny),
            buf(halos, 2, 2, nx, ny),
            buf(halos, 2, 2, nx, ny),
            buf(2, 2, nx, ny),
            buf(STEPS, 2, 3, xb + 2, ny),
            buf(STEPS, 2, 3, xb + 2, ny),
            buf(STEPS, 3, xb, zb, ny),
            buf(3, xb, zb, ny),
            buf(STEPS, 3, xb, zb, ny),
            buf(groups, 3, xb, zb, ny),
            buf(STEPS, groups, 3, xb, zb, ny),
            buf(STEPS, groups, 3, xb, zb, ny),
            buf(STEPS, groups, 3, xb, zb, ny),
            buf(STEPS, groups, 3, xb, zb, ny),
            buf(STEPS, zb, ny),
            buf(STEPS, n_slab, zb, ny),
            sem(STEPS, groups),
            sem(STEPS, groups),
            sem(STEPS, groups),
            sem(STEPS, groups),
            sem(halos, 2, n_orb),
            sem(halos, 2, n_orb),
            sem(STEPS, 2),
            sem(STEPS, 2),
            sem(STEPS, groups),
            sem(STEPS, groups),
            sem(STEPS, groups),
            sem(STEPS, groups),
            sem(STEPS, n_slab),
            sem(STEPS, n_slab),
        ],
        compiler_params=pltpu.CompilerParams(
            collective_id=0, has_side_effects=True, vmem_limit_bytes=60 * 1024 * 1024
        ),
    )(orbitals, potential, occupation, e_field, a_field)
    e_next = half - wave_step * flow
    return (moved * scale, e_next, a_old - wave_step * e_next)


def solution(mesh):
    return jax.shard_map(
        per_device,
        mesh=mesh,
        in_specs=(
            P("orb", None, None, "slab", None),
            P(None, "slab", None),
            P("orb"),
            P(None, "orb", "slab", None),
            P(None, "orb", "slab", None),
        ),
        out_specs=(
            P("orb", None, None, "slab", None),
            P(None, "orb", "slab", None),
            P(None, "orb", "slab", None),
        ),
        check_vma=False,
    )
```

```python
import functools

import jax
import jax.numpy as jnp
from jax import lax
from jax.experimental import pallas as pl
from jax.experimental.pallas import tpu as pltpu
from jax.sharding import PartitionSpec as P

TERMS = 4
STEPS = 2

time_step = 0.3
wave_step = 0.5
epsilon = 1e-06

MESH = pl.DeviceIdType.MESH
F32 = jnp.float32


def kernel(
    n_orb,
    n_slab,
    orb_ref,
    pot_ref,
    occ_ref,
    e_ref,
    a_ref,
    out_ref,
    scale_ref,
    half_ref,
    flow_ref,
    aold_ref,
    ta,
    tb,
    tot,
    w3,
    af,
    sb,
    hz,
    hs,
    azs,
    azr,
    enew,
    ekeep,
    anew,
    jmine,
    jsend,
    prx,
    jsum,
    rsx,
    nbs,
    nbr,
    ag_s,
    ag_r,
    fw_s,
    fw_r,
    hz_s,
    hz_r,
    az_s,
    az_r,
    pr_s,
    pr_r,
    rs_s,
    rs_r,
    nb_s,
    nb_r,
):
    groups = n_orb // 2
    _, _, nx, zb, ny = orb_ref.shape
    xb = a_ref.shape[1]
    xc = 8 if nx % 8 == 0 and xb % 8 == 0 else xb
    cells = nx * zb * n_slab * ny
    me = lax.axis_index("orb")
    me_s = lax.axis_index("slab")
    me_g = me // 2
    core = me % 2
    partner = me_g * 2 + (1 - core)
    has = (me_s > 0, me_s < n_slab - 1)
    nbr_dev = (me_s - 1, me_s + 1)

    barrier = pltpu.get_barrier_semaphore()

    def greet(o, s):
        pl.semaphore_signal(barrier, inc=1, device_id=(o, s), device_id_type=MESH)

    relay = groups == 4

    def group(d, c=None):
        c = core if c is None else c
        if not relay:
            return lax.rem(me_g + d, groups)
        by_x, by_y = me_g + 1 - 2 * (me_g % 2), lax.rem(me_g + 2, 4)
        return (
            me_g,
            by_x * (1 - c) + by_y * c,
            by_y * (1 - c) + by_x * c,
            3 - me_g,
        )[d]

    def source(d, c=None):
        if relay:
            return group(d, c)
        return lax.rem(me_g + groups - d, groups)

    greet(partner, me_s)
    for d in range(1, groups):
        greet(group(d) * 2 + core, me_s)
    for d in range(1, n_slab):
        greet(me, lax.rem(me_s + d, n_slab))

    row = lax.broadcasted_iota(jnp.int32, (1, zb, ny), 1)
    lane = lax.broadcasted_iota(jnp.int32, (1, zb, ny), 2)
    edge = (row == 0, row == zb - 1)
    first_lane, last_lane = lane == 0, lane == ny - 1
    sends = []

    def remote(src, dst, ss, rs, o, s):
        return pltpu.make_async_remote_copy(
            src_ref=src, dst_ref=dst, send_sem=ss, recv_sem=rs, device_id=(o, s), device_id_type=MESH
        )

    def y_next(v):
        return jnp.where(last_lane, 0.0, pltpu.roll(v, ny - 1, 2))

    def y_prev(v):
        return jnp.where(first_lane, 0.0, pltpu.roll(v, 1, 2))

    def z_next(v, halo=0.0):
        return jnp.where(edge[1], halo, pltpu.roll(v, zb - 1, 1))

    def z_prev(v, halo=0.0):
        return jnp.where(edge[0], halo, pltpu.roll(v, 1, 1))

    def rows_of(o):
        return pl.ds(o * xb, xb)

    def halo_copy(h, side, o):
        return remote(
            sb.at[h, side, :, rows_of(o)],
            hz.at[h, 1 - side, :, rows_of(o)],
            hz_s.at[h, side, o],
            hz_r.at[h, 1 - side, o],
            me,
            nbr_dev[side],
        )

    def send_halo(h, o):
        for side in range(2):

            @pl.when(has[side])
            def _():
                halo_copy(h, side, o).start()

    def wait_halo(h, o):
        for side in range(2):

            @pl.when(has[side])
            def _():
                remote(
                    sb.at[h, side, :, rows_of(o)],
                    hz.at[h, side, :, rows_of(o)],
                    hz_s.at[h, side, o],
                    hz_r.at[h, side, o],
                    me,
                    nbr_dev[side],
                ).wait_recv()

    def wait_halo_sent(h, o):
        for side in range(2):

            @pl.when(has[side])
            def _():
                halo_copy(h, side, o).wait_send()

    zero_x = jnp.zeros((zb, ny), F32)
    for buf in (ta, tb, tot):
        for part in range(2):
            buf[part, 0] = zero_x
            buf[part, nx + 1] = zero_x
    for step in range(STEPS):
        for comp in range(3):
            af[step, comp, 0] = zero_x
            af[step, comp, nx + 1] = zero_x

    def load_start(o, carry):
        for i in range(xb // xc):
            x = o * xb + i * xc
            for part in range(2):
                v = orb_ref[0, part, pl.ds(x, xc)]
                ta[part, pl.ds(1 + x, xc)] = v
                sb[0, 0, part, pl.ds(x, xc)] = v[:, 0, :]
                sb[0, 1, part, pl.ds(x, xc)] = v[:, zb - 1, :]
        send_halo(0, o)
        return carry

    for side in range(2):

        @pl.when(jnp.logical_not(has[side]))
        def _():
            for h in range(STEPS * (TERMS + 1)):
                hz[h, side] = jnp.zeros(hz.shape[2:], F32)
            for step in range(STEPS):
                azr[step, side] = jnp.zeros(azr.shape[2:], F32)

    pl.semaphore_wait(barrier, 1 + (groups - 1) + (n_slab - 1))

    def block(o):
        return pl.ds(1 + o * xb, xb)

    def gather_fields(step, src):
        for d in range(1, 3 if relay else groups):
            c = remote(src, af.at[step, :, block(me)], ag_s.at[step, d], ag_r.at[step, d], group(d) * 2 + core, me_s)
            c.start()
            sends.append(c)
        c = remote(src, af.at[step, :, block(me)], fw_s.at[step, 0], fw_r.at[step, 0], partner, me_s)
        c.start()
        sends.append(c)

    def weigh(step, o):
        def rows(i, carry):
            x = o * xb + i * xc
            a = [af[step, comp, pl.ds(1 + x, xc)] for comp in range(3)]
            w3[pl.ds(x, xc)] = (
                pot_ref[pl.ds(x, xc)] + 0.5 * (a[0] * a[0] + a[1] * a[1] + a[2] * a[2]) + 3.0
            )
            return carry

        lax.fori_loop(0, xb // xc, rows, 0)

    def finish_gather(step, src, use):
        for comp in range(3):
            af[step, comp, block(me)] = src[comp]
        weigh(step, me)
        use(me)
        for d in (2, 1, 3) if relay else range(1, groups):
            o = source(d) * 2 + core
            remote(
                src, af.at[step, :, block(o)], ag_s.at[step, d], ag_r.at[step, d], group(d) * 2 + core, me_s
            ).wait_recv()
            if relay and d == 2:
                c = remote(
                    af.at[step, :, block(o)],
                    af.at[step, :, block(o)],
                    ag_s.at[step, 3],
                    ag_r.at[step, 3],
                    group(1) * 2 + core,
                    me_s,
                )
                c.start()
                sends.append(c)
            c = remote(
                af.at[step, :, block(o)], af.at[step, :, block(o)], fw_s.at[step, d], fw_r.at[step, d], partner, me_s
            )
            c.start()
            sends.append(c)
            weigh(step, o)
            use(o)
        for d in (0, 2, 1, 3) if relay else range(groups):
            o = source(d, 1 - core) * 2 + (1 - core)
            remote(
                af.at[step, :, block(o)], af.at[step, :, block(o)], fw_s.at[step, d], fw_r.at[step, d], partner, me_s
            ).wait_recv()
            weigh(step, o)
            use(o)

    def az_copy(step, side):
        return remote(
            azs.at[step, side],
            azr.at[step, 1 - side],
            az_s.at[step, side],
            az_r.at[step, 1 - side],
            me,
            nbr_dev[side],
        )

    def send_az(step):
        for comp in range(3):
            v = af[step, comp, pl.ds(me * xb, xb + 2)]
            azs[step, 0, comp] = v[:, 0, :]
            azs[step, 1, comp] = v[:, zb - 1, :]
        for side in range(2):

            @pl.when(has[side])
            def _():
                az_copy(step, side).start()

    def half_fields(step, e_src):
        for side in range(2):

            @pl.when(has[side])
            def _():
                remote(
                    azs.at[step, side],
                    azr.at[step, side],
                    az_s.at[step, side],
                    az_r.at[step, side],
                    me,
                    nbr_dev[side],
                ).wait_recv()

        def rows(i, carry):
            x = me * xb + 1 + i

            def at(comp, dx):
                return af[step, comp, pl.ds(x + dx, 1)]

            def up(comp, dx):
                return z_next(at(comp, dx), azr[step, 1, comp, pl.ds(1 + i + dx, 1)][:, None, :])

            def down(comp, dx):
                return z_prev(at(comp, dx), azr[step, 0, comp, pl.ds(1 + i + dx, 1)][:, None, :])

            ax, ay, az = at(0, 0), at(1, 0), at(2, 0)
            ax_m, ay_p, az_p = at(0, -1), at(1, 1), at(2, 1)
            c_x = (
                (ay_p - ay - y_prev(ay_p) + y_prev(ay))
                + (az_p - az - down(2, 1) + down(2, 0))
                - (y_next(ax) + y_prev(ax) + up(0, 0) + down(0, 0) - 4.0 * ax)
            )
            c_y = (
                (y_next(ax) - ax - y_next(ax_m) + ax_m)
                + (y_next(az) - az - y_next(down(2, 0)) + down(2, 0))
                - (ay_p + at(1, -1) + up(1, 0) + down(1, 0) - 4.0 * ay)
            )
            c_z = (
                (up(0, 0) - ax - up(0, -1) + ax_m)
                + (up(1, 0) - ay - y_prev(up(1, 0)) + y_prev(ay))
                - (az_p + at(2, -1) + y_next(az) + y_prev(az) - 4.0 * az)
            )
            for comp, c in enumerate((c_x, c_y, c_z)):
                enew[step, comp, pl.ds(i, 1)] = e_src[comp, pl.ds(i, 1)] + wave_step * c
            return carry

        lax.fori_loop(0, xb, rows, 0)

    def term_block(step, order, t, tn, o, acc):
        f = time_step / order
        base = step * (TERMS + 1)
        h_in, h_out = base + order - 1, base + order
        if h_in != TERMS + 1:
            wait_halo(h_in, o)

        def rows(i, acc):
            x = o * xb + i * xc
            field = [af[step, comp, pl.ds(1 + x, xc)] for comp in range(3)]
            wt = w3[pl.ds(x, xc)]
            mid, total, drift = [], [], []
            for part in range(2):
                v = t[part, pl.ds(1 + x, xc)]
                xp, xm = t[part, pl.ds(2 + x, xc)], t[part, pl.ds(x, xc)]
                yp, ym = y_next(v), y_prev(v)
                zp = z_next(v, hz[h_in, 1, part, pl.ds(x, xc)][:, None, :])
                zm = z_prev(v, hz[h_in, 0, part, pl.ds(x, xc)][:, None, :])
                mid.append(v)
                total.append((xp + xm) + (yp + ym) + (zp + zm))
                drift.append(field[0] * (xp - xm) + field[1] * (yp - ym) + field[2] * (zp - zm))
            new_p = f * (wt * mid[1]) - (0.5 * f) * (total[1] + drift[0])
            new_q = (0.5 * f) * (total[0] - drift[1]) - f * (wt * mid[0])
            for part, new in enumerate((new_p, new_q)):
                sb[h_out, 0, part, pl.ds(x, xc)] = new[:, 0, :]
                sb[h_out, 1, part, pl.ds(x, xc)] = new[:, zb - 1, :]
                if order == 1:
                    s = mid[part] + new
                else:
                    s = tot[part, pl.ds(1 + x, xc)] + new
                tot[part, pl.ds(1 + x, xc)] = s
                if order < TERMS:
                    tn[part, pl.ds(1 + x, xc)] = new
                else:
                    acc = acc + jnp.sum(s * s, axis=0)
            return acc

        acc = lax.fori_loop(0, xb // xc, rows, acc)
        send_halo(h_out, o)
        return acc

    def current(step, o, s2h, dst):
        base = step * (TERMS + 1)
        wait_halo(base + TERMS, o)
        for side in range(2):
            for part in range(2):
                total = hz[base, side, part, rows_of(o)]
                for k in range(1, TERMS + 1):
                    total = total + hz[base + k, side, part, rows_of(o)]
                hs[side, part, rows_of(o)] = total

        def rows(i, carry):
            x = o * xb + i * xc
            mids, diffs = [], []
            for part in range(2):
                v = tot[part, pl.ds(1 + x, xc)]
                low = hs[0, part, pl.ds(x, xc)][:, None, :]
                high = hs[1, part, pl.ds(x, xc)][:, None, :]
                mids.append(v)
                diffs.append(
                    (
                        tot[part, pl.ds(2 + x, xc)] - tot[part, pl.ds(x, xc)],
                        y_next(v) - y_prev(v),
                        z_next(v, high) - z_prev(v, low),
                    )
                )
            u, w = mids
            density = 2.0 * (u * u + w * w)
            for comp in range(3):
                a = af[step, comp, pl.ds(1 + x, xc)]
                j = u * diffs[1][comp] - w * diffs[0][comp] + a * density
                dst[comp, pl.ds(i * xc, xc)] = j if s2h is None else s2h * j
            return carry

        lax.fori_loop(0, xb // xc, rows, 0)

    none = jnp.zeros((zb, ny), F32)
    order_d = [3, 1, 2, 0] if relay else list(range(1, groups)) + [0]
    gather_fields(0, a_ref)
    lax.fori_loop(0, n_orb, load_start, 0)
    for step in range(STEPS):
        base = step * (TERMS + 1)
        a_src = a_ref if step == 0 else anew.at[step - 1]
        e_src = e_ref if step == 0 else ekeep
        finish_gather(step, a_src, lambda o: term_block(step, 1, ta, tb, o, none))
        send_az(step)
        t, tn = tb, ta
        for order in range(2, TERMS):
            lax.fori_loop(
                0, n_orb, lambda o, acc: term_block(step, order, t, tn, o, acc), none
            )
            t, tn = tn, t

        norm_tile = none
        for c in (1 - core, core):
            for d in order_d:
                norm_tile = term_block(step, TERMS, t, tn, group(d, c) * 2 + c, norm_tile)
        nbs[step] = norm_tile
        for d in range(1, n_slab):
            c = remote(
                nbs.at[step], nbr.at[step, d], nb_s.at[step, d], nb_r.at[step, d], me, lax.rem(me_s + d, n_slab)
            )
            c.start()
            sends.append(c)
        for d in order_d:
            current(step, group(d, 1 - core) * 2 + (1 - core), None, jmine.at[d])
        for d in range(1, n_slab):
            remote(nbs.at[step], nbr.at[step, d], nb_s.at[step, d], nb_r.at[step, d], me, me_s).wait_recv()
            norm_tile = norm_tile + nbr[step, d]
        norm = jnp.sum(jnp.sum(norm_tile, axis=0, keepdims=True), axis=1, keepdims=True)
        scale = jnp.broadcast_to(1.0 / jnp.sqrt(norm / cells + epsilon), (zb, ny))
        s2h = (scale * scale * (0.5 * (occ_ref[0] * (1.0 / n_orb))))[None]
        for d in order_d:
            for comp in range(3):
                jsend[step, d, comp] = s2h * jmine[d, comp]
            c = remote(
                jsend.at[step, d], prx.at[step, d], pr_s.at[step, d], pr_r.at[step, d], partner, me_s
            )
            c.start()
            sends.append(c)
        for d in order_d:
            current(step, group(d) * 2 + core, s2h, jmine.at[d])
            remote(
                jsend.at[step, d], prx.at[step, d], pr_s.at[step, d], pr_r.at[step, d], partner, me_s
            ).wait_recv()
            if relay and d == 2:
                remote(
                    jsum.at[step, 3], rsx.at[step, 3], rs_s.at[step, 3], rs_r.at[step, 3], partner, me_s
                ).wait_recv()
            for comp in range(3):
                total = jmine[d, comp] + prx[step, d, comp]
                if relay and d == 2:
                    total = total + rsx[step, 3, comp]
                jsum[step, d, comp] = total
            if d:
                to = group(1 if relay and d == 3 else d) * 2 + core
                c = remote(
                    jsum.at[step, d], rsx.at[step, d], rs_s.at[step, d], rs_r.at[step, d], to, me_s
                )
                c.start()
                sends.append(c)

        def rescale(i, carry):
            x = i * xc
            for part in range(2):
                v = tot[part, pl.ds(1 + x, xc)]
                if step == STEPS - 1:
                    out_ref[0, part, pl.ds(x, xc)] = v
                else:
                    ta[part, pl.ds(1 + x, xc)] = scale[None] * v
            return carry

        lax.fori_loop(0, nx // xc, rescale, 0)
        half_fields(step, e_src)
        if step < STEPS - 1:
            for side in range(2):
                for part in range(2):
                    hz[base + TERMS + 1, side, part] = scale[0:1] * hs[side, part]
        arriving = range(1, 3 if relay else groups)
        for d in arriving:
            remote(
                jsum.at[step, d], rsx.at[step, d], rs_s.at[step, d], rs_r.at[step, d], partner, me_s
            ).wait_recv()

        for comp in range(3):
            flow = jsum[step, 0, comp]
            for d in arriving:
                flow = flow + rsx[step, d, comp]
            if step == STEPS - 1:
                half_ref[comp] = enew[step, comp]
                flow_ref[comp] = flow
                aold_ref[comp] = a_src[comp]
            else:
                e = enew[step, comp] - wave_step * flow
                ekeep[comp] = e
                anew[step, comp] = a_src[comp] - wave_step * e
        if step < STEPS - 1:
            gather_fields(step + 1, anew.at[step])
        else:
            scale_ref[...] = scale

    for c in sends:
        c.wait_send()
    for h in range(STEPS * (TERMS + 1)):
        if h != TERMS + 1:
            lax.fori_loop(0, n_orb, lambda o, carry: (wait_halo_sent(h, o), carry)[1], 0)
    for step in range(STEPS):
        for side in range(2):

            @pl.when(has[side])
            def _():
                az_copy(step, side).wait_send()


def per_device(orbitals, potential, occupation, e_field, a_field):
    n_orb, n_slab = lax.axis_size("orb"), lax.axis_size("slab")
    _, _, nx, zb, ny = orbitals.shape
    xb = a_field.shape[1]
    groups = n_orb // 2
    halos = STEPS * (TERMS + 1)
    vmem = pl.BlockSpec(memory_space=pltpu.VMEM)

    def sem(*shape):
        return pltpu.SemaphoreType.DMA(shape)

    def buf(*shape):
        return pltpu.VMEM(shape, F32)

    moved, scale, half, flow, a_old = pl.pallas_call(
        functools.partial(kernel, n_orb, n_slab),
        out_shape=(
            jax.ShapeDtypeStruct(orbitals.shape, F32),
            jax.ShapeDtypeStruct((zb, ny), F32),
            jax.ShapeDtypeStruct(e_field.shape, F32),
            jax.ShapeDtypeStruct(e_field.shape, F32),
            jax.ShapeDtypeStruct(e_field.shape, F32),
        ),
        in_specs=[vmem, vmem, pl.BlockSpec(memory_space=pltpu.SMEM), vmem, vmem],
        out_specs=(vmem,) * 5,
        scratch_shapes=[
            buf(2, nx + 2, zb, ny),
            buf(2, nx + 2, zb, ny),
            buf(2, nx + 2, zb, ny),
            buf(nx, zb, ny),
            buf(STEPS, 3, nx + 2, zb, ny),
            buf(halos, 2, 2, nx, ny),
            buf(halos, 2, 2, nx, ny),
            buf(2, 2, nx, ny),
            buf(STEPS, 2, 3, xb + 2, ny),
            buf(STEPS, 2, 3, xb + 2, ny),
            buf(STEPS, 3, xb, zb, ny),
            buf(3, xb, zb, ny),
            buf(STEPS, 3, xb, zb, ny),
            buf(groups, 3, xb, zb, ny),
            buf(STEPS, groups, 3, xb, zb, ny),
            buf(STEPS, groups, 3, xb, zb, ny),
            buf(STEPS, groups, 3, xb, zb, ny),
            buf(STEPS, groups, 3, xb, zb, ny),
            buf(STEPS, zb, ny),
            buf(STEPS, n_slab, zb, ny),
            sem(STEPS, groups),
            sem(STEPS, groups),
            sem(STEPS, groups),
            sem(STEPS, groups),
            sem(halos, 2, n_orb),
            sem(halos, 2, n_orb),
            sem(STEPS, 2),
            sem(STEPS, 2),
            sem(STEPS, groups),
            sem(STEPS, groups),
            sem(STEPS, groups),
            sem(STEPS, groups),
            sem(STEPS, n_slab),
            sem(STEPS, n_slab),
        ],
        compiler_params=pltpu.CompilerParams(
            collective_id=0, has_side_effects=True, vmem_limit_bytes=60 * 1024 * 1024
        ),
    )(orbitals, potential, occupation, e_field, a_field)
    e_next = half - wave_step * flow
    return (moved * scale, e_next, a_old - wave_step * e_next)


def solution(mesh):
    return jax.shard_map(
        per_device,
        mesh=mesh,
        in_specs=(
            P("orb", None, None, "slab", None),
            P(None, "slab", None),
            P("orb"),
            P(None, "orb", "slab", None),
            P(None, "orb", "slab", None),
        ),
        out_specs=(
            P("orb", None, None, "slab", None),
            P(None, "orb", "slab", None),
            P(None, "orb", "slab", None),
        ),
        check_vma=False,
    )
```

```python
import functools

import jax
import jax.numpy as jnp
from jax import lax
from jax.experimental import pallas as pl
from jax.experimental.pallas import tpu as pltpu
from jax.sharding import PartitionSpec as P

TERMS = 4
STEPS = 2

time_step = 0.3
wave_step = 0.5
epsilon = 1e-06

MESH = pl.DeviceIdType.MESH
F32 = jnp.float32


def kernel(
    n_orb,
    n_slab,
    orb_ref,
    pot_ref,
    occ_ref,
    e_ref,
    a_ref,
    out_ref,
    scale_ref,
    eout_ref,
    aout_ref,
    ta,
    tb,
    tot,
    w3,
    af,
    sb,
    hz,
    hs,
    azs,
    azr,
    enew,
    ekeep,
    anew,
    jmine,
    jsend,
    prx,
    jsum,
    rsx,
    nbs,
    nbr,
    ag_s,
    ag_r,
    fw_s,
    fw_r,
    hz_s,
    hz_r,
    az_s,
    az_r,
    pr_s,
    pr_r,
    rs_s,
    rs_r,
    nb_s,
    nb_r,
):
    groups = n_orb // 2
    _, _, nx, zb, ny = orb_ref.shape
    xb = a_ref.shape[1]
    xc = 8 if nx % 8 == 0 and xb % 8 == 0 else xb
    cells = nx * zb * n_slab * ny
    me = lax.axis_index("orb")
    me_s = lax.axis_index("slab")
    me_g = me // 2
    core = me % 2
    partner = me_g * 2 + (1 - core)
    has = (me_s > 0, me_s < n_slab - 1)
    nbr_dev = (me_s - 1, me_s + 1)

    barrier = pltpu.get_barrier_semaphore()

    def greet(o, s):
        pl.semaphore_signal(barrier, inc=1, device_id=(o, s), device_id_type=MESH)

    relay = groups == 4

    def group(d, c=None):
        c = core if c is None else c
        if not relay:
            return lax.rem(me_g + d, groups)
        by_x, by_y = me_g + 1 - 2 * (me_g % 2), lax.rem(me_g + 2, 4)
        return (
            me_g,
            by_x * (1 - c) + by_y * c,
            by_y * (1 - c) + by_x * c,
            3 - me_g,
        )[d]

    def source(d, c=None):
        if relay:
            return group(d, c)
        return lax.rem(me_g + groups - d, groups)

    greet(partner, me_s)
    for d in range(1, groups):
        greet(group(d) * 2 + core, me_s)
    for d in range(1, n_slab):
        greet(me, lax.rem(me_s + d, n_slab))

    row = lax.broadcasted_iota(jnp.int32, (1, zb, ny), 1)
    lane = lax.broadcasted_iota(jnp.int32, (1, zb, ny), 2)
    edge = (row == 0, row == zb - 1)
    first_lane, last_lane = lane == 0, lane == ny - 1
    sends = []

    def remote(src, dst, ss, rs, o, s):
        return pltpu.make_async_remote_copy(
            src_ref=src, dst_ref=dst, send_sem=ss, recv_sem=rs, device_id=(o, s), device_id_type=MESH
        )

    def y_next(v):
        return jnp.where(last_lane, 0.0, pltpu.roll(v, ny - 1, 2))

    def y_prev(v):
        return jnp.where(first_lane, 0.0, pltpu.roll(v, 1, 2))

    def z_next(v, halo=0.0):
        return jnp.where(edge[1], halo, pltpu.roll(v, zb - 1, 1))

    def z_prev(v, halo=0.0):
        return jnp.where(edge[0], halo, pltpu.roll(v, 1, 1))

    def rows_of(o):
        return pl.ds(o * xb, xb)

    def halo_copy(h, side, o):
        return remote(
            sb.at[h, side, :, rows_of(o)],
            hz.at[h, 1 - side, :, rows_of(o)],
            hz_s.at[h, side, o],
            hz_r.at[h, 1 - side, o],
            me,
            nbr_dev[side],
        )

    def send_halo(h, o):
        for side in range(2):

            @pl.when(has[side])
            def _():
                halo_copy(h, side, o).start()

    def wait_halo(h, o):
        for side in range(2):

            @pl.when(has[side])
            def _():
                remote(
                    sb.at[h, side, :, rows_of(o)],
                    hz.at[h, side, :, rows_of(o)],
                    hz_s.at[h, side, o],
                    hz_r.at[h, side, o],
                    me,
                    nbr_dev[side],
                ).wait_recv()

    def wait_halo_sent(h, o):
        for side in range(2):

            @pl.when(has[side])
            def _():
                halo_copy(h, side, o).wait_send()

    zero_x = jnp.zeros((zb, ny), F32)
    for buf in (ta, tb, tot):
        for part in range(2):
            buf[part, 0] = zero_x
            buf[part, nx + 1] = zero_x
    for step in range(STEPS):
        for comp in range(3):
            af[step, comp, 0] = zero_x
            af[step, comp, nx + 1] = zero_x

    def load_start(j, carry):
        o = lax.rem(me + j, n_orb)
        for i in range(xb // xc):
            x = o * xb + i * xc
            for part in range(2):
                v = orb_ref[0, part, pl.ds(x, xc)]
                ta[part, pl.ds(1 + x, xc)] = v
                sb[0, 0, part, pl.ds(x, xc)] = v[:, 0, :]
                sb[0, 1, part, pl.ds(x, xc)] = v[:, zb - 1, :]
        send_halo(0, o)
        return carry

    for side in range(2):

        @pl.when(jnp.logical_not(has[side]))
        def _():
            for h in range(STEPS * (TERMS + 1)):
                hz[h, side] = jnp.zeros(hz.shape[2:], F32)
            for step in range(STEPS):
                azr[step, side] = jnp.zeros(azr.shape[2:], F32)

    pl.semaphore_wait(barrier, 1 + (groups - 1) + (n_slab - 1))

    def block(o):
        return pl.ds(1 + o * xb, xb)

    def gather_fields(step, src):
        for d in range(1, 3 if relay else groups):
            c = remote(src, af.at[step, :, block(me)], ag_s.at[step, d], ag_r.at[step, d], group(d) * 2 + core, me_s)
            c.start()
            sends.append(c)
        c = remote(src, af.at[step, :, block(me)], fw_s.at[step, 0], fw_r.at[step, 0], partner, me_s)
        c.start()
        sends.append(c)

    def weigh(step, o):
        def rows(i, carry):
            x = o * xb + i * xc
            a = [af[step, comp, pl.ds(1 + x, xc)] for comp in range(3)]
            w3[pl.ds(x, xc)] = (
                pot_ref[pl.ds(x, xc)] + 0.5 * (a[0] * a[0] + a[1] * a[1] + a[2] * a[2]) + 3.0
            )
            return carry

        lax.fori_loop(0, xb // xc, rows, 0)

    def finish_gather(step, src, use):
        for comp in range(3):
            af[step, comp, block(me)] = src[comp]
        pending = me
        for d in (2, 1, 3) if relay else range(1, groups):
            o = source(d) * 2 + core
            remote(
                src, af.at[step, :, block(o)], ag_s.at[step, d], ag_r.at[step, d], group(d) * 2 + core, me_s
            ).wait_recv()
            if relay and d == 2:
                c = remote(
                    af.at[step, :, block(o)],
                    af.at[step, :, block(o)],
                    ag_s.at[step, 3],
                    ag_r.at[step, 3],
                    group(1) * 2 + core,
                    me_s,
                )
                c.start()
                sends.append(c)
            c = remote(
                af.at[step, :, block(o)], af.at[step, :, block(o)], fw_s.at[step, d], fw_r.at[step, d], partner, me_s
            )
            c.start()
            sends.append(c)
            weigh(step, pending)
            use(pending)
            pending = o
        weigh(step, pending)
        use(pending)
        for d in (0, 2, 1, 3) if relay else range(groups):
            o = source(d, 1 - core) * 2 + (1 - core)
            remote(
                af.at[step, :, block(o)], af.at[step, :, block(o)], fw_s.at[step, d], fw_r.at[step, d], partner, me_s
            ).wait_recv()
            weigh(step, o)
            use(o)

    def az_copy(step, side):
        return remote(
            azs.at[step, side],
            azr.at[step, 1 - side],
            az_s.at[step, side],
            az_r.at[step, 1 - side],
            me,
            nbr_dev[side],
        )

    def send_az(step):
        for comp in range(3):
            v = af[step, comp, pl.ds(me * xb, xb + 2)]
            azs[step, 0, comp] = v[:, 0, :]
            azs[step, 1, comp] = v[:, zb - 1, :]
        for side in range(2):

            @pl.when(has[side])
            def _():
                az_copy(step, side).start()

    def half_fields(step, e_src):
        for side in range(2):

            @pl.when(has[side])
            def _():
                remote(
                    azs.at[step, side],
                    azr.at[step, side],
                    az_s.at[step, side],
                    az_r.at[step, side],
                    me,
                    nbr_dev[side],
                ).wait_recv()

        def rows(i, carry):
            x = me * xb + 1 + i

            def at(comp, dx):
                return af[step, comp, pl.ds(x + dx, 1)]

            def up(comp, dx):
                return z_next(at(comp, dx), azr[step, 1, comp, pl.ds(1 + i + dx, 1)][:, None, :])

            def down(comp, dx):
                return z_prev(at(comp, dx), azr[step, 0, comp, pl.ds(1 + i + dx, 1)][:, None, :])

            ax, ay, az = at(0, 0), at(1, 0), at(2, 0)
            ax_m, ay_p, az_p = at(0, -1), at(1, 1), at(2, 1)
            c_x = (
                (ay_p - ay - y_prev(ay_p) + y_prev(ay))
                + (az_p - az - down(2, 1) + down(2, 0))
                - (y_next(ax) + y_prev(ax) + up(0, 0) + down(0, 0) - 4.0 * ax)
            )
            c_y = (
                (y_next(ax) - ax - y_next(ax_m) + ax_m)
                + (y_next(az) - az - y_next(down(2, 0)) + down(2, 0))
                - (ay_p + at(1, -1) + up(1, 0) + down(1, 0) - 4.0 * ay)
            )
            c_z = (
                (up(0, 0) - ax - up(0, -1) + ax_m)
                + (up(1, 0) - ay - y_prev(up(1, 0)) + y_prev(ay))
                - (az_p + at(2, -1) + y_next(az) + y_prev(az) - 4.0 * az)
            )
            for comp, c in enumerate((c_x, c_y, c_z)):
                enew[step, comp, pl.ds(i, 1)] = e_src[comp, pl.ds(i, 1)] + wave_step * c
            return carry

        lax.fori_loop(0, xb, rows, 0)

    def term_block(step, order, t, tn, o, acc):
        f = time_step / order
        base = step * (TERMS + 1)
        h_in, h_out = base + order - 1, base + order
        if h_in != TERMS + 1:
            wait_halo(h_in, o)

        def rows(i, acc):
            x = o * xb + i * xc
            field = [af[step, comp, pl.ds(1 + x, xc)] for comp in range(3)]
            wt = w3[pl.ds(x, xc)]
            mid, total, drift = [], [], []
            for part in range(2):
                v = t[part, pl.ds(1 + x, xc)]
                xp, xm = t[part, pl.ds(2 + x, xc)], t[part, pl.ds(x, xc)]
                yp, ym = y_next(v), y_prev(v)
                zp = z_next(v, hz[h_in, 1, part, pl.ds(x, xc)][:, None, :])
                zm = z_prev(v, hz[h_in, 0, part, pl.ds(x, xc)][:, None, :])
                mid.append(v)
                total.append((xp + xm) + (yp + ym) + (zp + zm))
                drift.append(field[0] * (xp - xm) + field[1] * (yp - ym) + field[2] * (zp - zm))
            new_p = f * (wt * mid[1]) - (0.5 * f) * (total[1] + drift[0])
            new_q = (0.5 * f) * (total[0] - drift[1]) - f * (wt * mid[0])
            for part, new in enumerate((new_p, new_q)):
                sb[h_out, 0, part, pl.ds(x, xc)] = new[:, 0, :]
                sb[h_out, 1, part, pl.ds(x, xc)] = new[:, zb - 1, :]
                if order == 1:
                    s = mid[part] + new
                else:
                    s = tot[part, pl.ds(1 + x, xc)] + new
                tot[part, pl.ds(1 + x, xc)] = s
                if order < TERMS:
                    tn[part, pl.ds(1 + x, xc)] = new
                else:
                    acc = acc + jnp.sum(s * s, axis=0)
            return acc

        acc = lax.fori_loop(0, xb // xc, rows, acc)
        send_halo(h_out, o)
        return acc

    def current(step, o, s2h, dst):
        base = step * (TERMS + 1)
        wait_halo(base + TERMS, o)
        for side in range(2):
            for part in range(2):
                total = hz[base, side, part, rows_of(o)]
                for k in range(1, TERMS + 1):
                    total = total + hz[base + k, side, part, rows_of(o)]
                hs[side, part, rows_of(o)] = total

        def rows(i, carry):
            x = o * xb + i * xc
            mids, diffs = [], []
            for part in range(2):
                v = tot[part, pl.ds(1 + x, xc)]
                low = hs[0, part, pl.ds(x, xc)][:, None, :]
                high = hs[1, part, pl.ds(x, xc)][:, None, :]
                mids.append(v)
                diffs.append(
                    (
                        tot[part, pl.ds(2 + x, xc)] - tot[part, pl.ds(x, xc)],
                        y_next(v) - y_prev(v),
                        z_next(v, high) - z_prev(v, low),
                    )
                )
            u, w = mids
            density = 2.0 * (u * u + w * w)
            for comp in range(3):
                a = af[step, comp, pl.ds(1 + x, xc)]
                j = u * diffs[1][comp] - w * diffs[0][comp] + a * density
                dst[comp, pl.ds(i * xc, xc)] = j if s2h is None else s2h * j
            return carry

        lax.fori_loop(0, xb // xc, rows, 0)

    none = jnp.zeros((zb, ny), F32)
    order_d = [3, 1, 2, 0] if relay else list(range(1, groups)) + [0]
    gather_fields(0, a_ref)
    lax.fori_loop(0, n_orb, load_start, 0)
    for step in range(STEPS):
        base = step * (TERMS + 1)
        a_src = a_ref if step == 0 else anew.at[step - 1]
        e_src = e_ref if step == 0 else ekeep
        finish_gather(step, a_src, lambda o: term_block(step, 1, ta, tb, o, none))
        send_az(step)
        t, tn = tb, ta
        for order in range(2, TERMS):
            lax.fori_loop(
                0, n_orb, lambda o, acc: term_block(step, order, t, tn, o, acc), none
            )
            t, tn = tn, t

        norm_tile = none
        for c in (1 - core, core):
            for d in order_d:
                norm_tile = term_block(step, TERMS, t, tn, group(d, c) * 2 + c, norm_tile)
        nbs[step] = norm_tile
        for d in range(1, n_slab):
            c = remote(
                nbs.at[step], nbr.at[step, d], nb_s.at[step, d], nb_r.at[step, d], me, lax.rem(me_s + d, n_slab)
            )
            c.start()
            sends.append(c)
        for d in order_d:
            current(step, group(d, 1 - core) * 2 + (1 - core), None, jmine.at[d])
        for d in range(1, n_slab):
            remote(nbs.at[step], nbr.at[step, d], nb_s.at[step, d], nb_r.at[step, d], me, me_s).wait_recv()
            norm_tile = norm_tile + nbr[step, d]
        norm = jnp.sum(jnp.sum(norm_tile, axis=0, keepdims=True), axis=1, keepdims=True)
        scale = jnp.broadcast_to(1.0 / jnp.sqrt(norm / cells + epsilon), (zb, ny))
        s2h = (scale * scale * (0.5 * (occ_ref[0] * (1.0 / n_orb))))[None]
        for d in order_d:
            for comp in range(3):
                jsend[step, d, comp] = s2h * jmine[d, comp]
            c = remote(
                jsend.at[step, d], prx.at[step, d], pr_s.at[step, d], pr_r.at[step, d], partner, me_s
            )
            c.start()
            sends.append(c)
        for d in order_d:
            current(step, group(d) * 2 + core, s2h, jmine.at[d])
            remote(
                jsend.at[step, d], prx.at[step, d], pr_s.at[step, d], pr_r.at[step, d], partner, me_s
            ).wait_recv()
            if relay and d == 2:
                remote(
                    jsum.at[step, 3], rsx.at[step, 3], rs_s.at[step, 3], rs_r.at[step, 3], partner, me_s
                ).wait_recv()
            for comp in range(3):
                total = jmine[d, comp] + prx[step, d, comp]
                if relay and d == 2:
                    total = total + rsx[step, 3, comp]
                jsum[step, d, comp] = total
            if d:
                to = group(1 if relay and d == 3 else d) * 2 + core
                c = remote(
                    jsum.at[step, d], rsx.at[step, d], rs_s.at[step, d], rs_r.at[step, d], to, me_s
                )
                c.start()
                sends.append(c)

        def rescale(i, carry):
            x = i * xc
            for part in range(2):
                v = tot[part, pl.ds(1 + x, xc)]
                if step == STEPS - 1:
                    out_ref[0, part, pl.ds(x, xc)] = v
                else:
                    ta[part, pl.ds(1 + x, xc)] = scale[None] * v
            return carry

        lax.fori_loop(0, nx // xc, rescale, 0)
        half_fields(step, e_src)
        if step < STEPS - 1:
            for side in range(2):
                for part in range(2):
                    hz[base + TERMS + 1, side, part] = scale[0:1] * hs[side, part]
        arriving = range(1, 3 if relay else groups)
        for d in arriving:
            remote(
                jsum.at[step, d], rsx.at[step, d], rs_s.at[step, d], rs_r.at[step, d], partner, me_s
            ).wait_recv()

        for comp in range(3):
            flow = jsum[step, 0, comp]
            for d in arriving:
                flow = flow + rsx[step, d, comp]
            e = enew[step, comp] - wave_step * flow
            a = a_src[comp] - wave_step * e
            if step == STEPS - 1:
                eout_ref[comp] = e
                aout_ref[comp] = a
            else:
                ekeep[comp] = e
                anew[step, comp] = a
        if step < STEPS - 1:
            gather_fields(step + 1, anew.at[step])
        else:
            scale_ref[...] = scale

    for c in sends:
        c.wait_send()
    for h in range(STEPS * (TERMS + 1)):
        if h != TERMS + 1:
            lax.fori_loop(0, n_orb, lambda o, carry: (wait_halo_sent(h, o), carry)[1], 0)
    for step in range(STEPS):
        for side in range(2):

            @pl.when(has[side])
            def _():
                az_copy(step, side).wait_send()


def per_device(orbitals, potential, occupation, e_field, a_field):
    n_orb, n_slab = lax.axis_size("orb"), lax.axis_size("slab")
    _, _, nx, zb, ny = orbitals.shape
    xb = a_field.shape[1]
    groups = n_orb // 2
    halos = STEPS * (TERMS + 1)
    vmem = pl.BlockSpec(memory_space=pltpu.VMEM)

    def sem(*shape):
        return pltpu.SemaphoreType.DMA(shape)

    def buf(*shape):
        return pltpu.VMEM(shape, F32)

    moved, scale, e_next, a_next = pl.pallas_call(
        functools.partial(kernel, n_orb, n_slab),
        out_shape=(
            jax.ShapeDtypeStruct(orbitals.shape, F32),
            jax.ShapeDtypeStruct((zb, ny), F32),
            jax.ShapeDtypeStruct(e_field.shape, F32),
            jax.ShapeDtypeStruct(e_field.shape, F32),
        ),
        in_specs=[vmem, vmem, pl.BlockSpec(memory_space=pltpu.SMEM), vmem, vmem],
        out_specs=(vmem,) * 4,
        scratch_shapes=[
            buf(2, nx + 2, zb, ny),
            buf(2, nx + 2, zb, ny),
            buf(2, nx + 2, zb, ny),
            buf(nx, zb, ny),
            buf(STEPS, 3, nx + 2, zb, ny),
            buf(halos, 2, 2, nx, ny),
            buf(halos, 2, 2, nx, ny),
            buf(2, 2, nx, ny),
            buf(STEPS, 2, 3, xb + 2, ny),
            buf(STEPS, 2, 3, xb + 2, ny),
            buf(STEPS, 3, xb, zb, ny),
            buf(3, xb, zb, ny),
            buf(STEPS, 3, xb, zb, ny),
            buf(groups, 3, xb, zb, ny),
            buf(STEPS, groups, 3, xb, zb, ny),
            buf(STEPS, groups, 3, xb, zb, ny),
            buf(STEPS, groups, 3, xb, zb, ny),
            buf(STEPS, groups, 3, xb, zb, ny),
            buf(STEPS, zb, ny),
            buf(STEPS, n_slab, zb, ny),
            sem(STEPS, groups),
            sem(STEPS, groups),
            sem(STEPS, groups),
            sem(STEPS, groups),
            sem(halos, 2, n_orb),
            sem(halos, 2, n_orb),
            sem(STEPS, 2),
            sem(STEPS, 2),
            sem(STEPS, groups),
            sem(STEPS, groups),
            sem(STEPS, groups),
            sem(STEPS, groups),
            sem(STEPS, n_slab),
            sem(STEPS, n_slab),
        ],
        compiler_params=pltpu.CompilerParams(
            collective_id=0, has_side_effects=True, vmem_limit_bytes=60 * 1024 * 1024
        ),
    )(orbitals, potential, occupation, e_field, a_field)
    return (moved * scale, e_next, a_next)


def solution(mesh):
    return jax.shard_map(
        per_device,
        mesh=mesh,
        in_specs=(
            P("orb", None, None, "slab", None),
            P(None, "slab", None),
            P("orb"),
            P(None, "orb", "slab", None),
            P(None, "orb", "slab", None),
        ),
        out_specs=(
            P("orb", None, None, "slab", None),
            P(None, "orb", "slab", None),
            P(None, "orb", "slab", None),
        ),
        check_vma=False,
    )
```
